256 devices in a mesh: ctx: 32 (over x, z_lo, core), head: 2 (over z_hi), tp: 4 (over y).
Axes of the slice: x: 4, y: 4, z: 8 (z_hi: 2, z_lo: 4; z = z_hi * 4 + z_lo), core: 2. Of those that a mesh axis runs over, the one named last changes fastest.
Arguments:
- text_states: bfloat16 [256, 8192], P(None, 'ctx'), may hold values from -6 to 6
- q_weight: bfloat16 [8192, 8192], P('ctx', ('head', 'tp')), may hold values from -0.0625 to 0.0625
- q_gain: float32 [128], replicated, may hold values from 0.1 to 1.9
- visual_key_cache: bfloat16 [16384, 1024], P('ctx', ('head', 'tp')), may hold values from -400 to 400
- visual_value_cache: bfloat16 [16384, 1024], P('ctx', ('head', 'tp')), may hold values from -6 to 6
- block_mask: int32 [256, 64], P(None, 'ctx'), may hold values from 0 to 1, as said below
- lengths: int32 [256], replicated, may hold values from 256 to 16384, as said below
- o_weight: bfloat16 [8192, 8192], P(('head', 'tp'), 'ctx'), may hold values from -0.59765625 to 0.59765625
Outputs:
- updated: bfloat16 [256, 8192], P(('head', 'tp'), 'ctx')
The draws below stay inside these ranges and needn't reach their ends.
Inputs may be any that keep to these rules, and one draw needn't show every extreme that they name: `block_mask`: segment 0 is visible to every row. `lengths`: some row sees all 16384 tokens.
All inputs are finite; a program needn't handle non-finite values.
Results may differ from the reference program's by a relative error of at most 0.0055.
Values may be sent and summed in bfloat16 or wider, within the bound.
A program may use at most 64 MiB of HBM per device.

```python
import jax
import jax.numpy as jnp
from jax import lax

D = 8192
QUERY_HEAD_COUNT = 64
KEY_VALUE_HEADS = 8
HEAD_SIZE = 128
TEXT = 256
VISUAL_PER_CTX = 512
SEG = 256
VISUAL_TOKENS = 16384
NSEG = 64
N_CTX = 32


def draw_visual_key_cache(key, part):
    initial_random_key = jax.random.fold_in(key, 11)
    random_base_seed = 2.0 * jax.random.truncated_normal(initial_random_key, -4.0, 4.0, (VISUAL_TOKENS, KEY_VALUE_HEADS * HEAD_SIZE), jnp.float32)
    result = random_base_seed
    return result.astype(jnp.bfloat16)


def draw_block_mask(key, part):
    initial_random_key = jax.random.fold_in(key, 21)
    visible = jax.random.randint(initial_random_key, (TEXT, NSEG), 0, 2).astype(jnp.int32)
    return visible.at[:, 0].set(1)


def draw_lengths(key, part):
    initial_random_key = jax.random.fold_in(key, 31)
    second_key = jax.random.fold_in(key, 32)
    drawn = jax.random.randint(initial_random_key, (TEXT,), SEG, VISUAL_TOKENS + 1).astype(jnp.int32)
    chosen = jax.random.randint(second_key, (), 0, TEXT)
    return drawn.at[chosen].set(VISUAL_TOKENS)


def shard_levels(key, shape, split, low, largest):
    factor_of, own = 1.0, jax.random.fold_in(key, 6)
    for dim, parts in split:
        heights = jnp.exp(jax.random.uniform(jax.random.fold_in(own, dim), (parts,), jnp.float32, low / len(split), largest / len(split)))
        factor_of = factor_of * jnp.repeat(heights, shape[dim] // parts).reshape([-1 if axis == dim else 1 for axis in range(len(shape))])
    return factor_of


def gaussian(rng, shape, width, reach, pieces=(), kind=jnp.bfloat16):
    values = jax.random.normal(rng, shape, jnp.float32) * width
    if len(pieces) > 0:
        values = shard_levels(rng, shape, pieces, -0.22, 0.18) * values
    return jnp.clip(values, min=-reach, max=reach).astype(kind)


def setup_inputs(seed: int = 0) -> dict:
    keys = jax.random.split(jax.random.key(seed), 9)
    return {
        "text_states": gaussian(keys[0], (TEXT, D), 1.0, 6.0, ((1, 32),)),
        "q_weight": gaussian(keys[1], (D, QUERY_HEAD_COUNT * HEAD_SIZE), D ** -0.5, 0.0625, ((0, 32), (1, 8))),
        "q_gain": jnp.clip(1.0 + 0.18 * jax.random.normal(keys[2], (HEAD_SIZE,), jnp.float32), 0.1, 1.9),
        "visual_key_cache": draw_visual_key_cache(jax.random.fold_in(keys[8], 71), 0),
        "visual_value_cache": gaussian(keys[4], (VISUAL_TOKENS, KEY_VALUE_HEADS * HEAD_SIZE), 1.0, 6.0, ((0, 32), (1, 8))),
        "block_mask": draw_block_mask(jax.random.fold_in(keys[8], 71), 0),
        "lengths": draw_lengths(jax.random.fold_in(keys[8], 71), 0),
        "o_weight": gaussian(keys[7], (QUERY_HEAD_COUNT * HEAD_SIZE, D), 0.1, 0.59765625, ((0, 8), (1, 32))),
    }


def reference(text_states, q_weight, q_gain, visual_key_cache, visual_value_cache, block_mask, lengths, o_weight):
    queries = jnp.dot(text_states, q_weight, preferred_element_type=jnp.float32)
    shaped = queries.reshape(TEXT, QUERY_HEAD_COUNT, HEAD_SIZE)
    mean_sq = lax.optimization_barrier(jnp.mean(shaped * shaped, axis=-1, keepdims=True))
    normed = (shaped * lax.rsqrt(mean_sq + 1e-05) * q_gain).astype(jnp.bfloat16)
    query_group_count = QUERY_HEAD_COUNT // KEY_VALUE_HEADS
    score_scale = 1.0 / HEAD_SIZE ** 0.5
    normed_wide = normed.astype(jnp.float32)

    def shard_step(state_carry, shard):
        key_block_offset = (shard * VISUAL_PER_CTX).astype(jnp.int32)
        key_tile_rows = lax.dynamic_slice_in_dim(visual_key_cache, key_block_offset, VISUAL_PER_CTX, 0).reshape(VISUAL_PER_CTX, KEY_VALUE_HEADS, HEAD_SIZE)
        value_tile_rows = lax.dynamic_slice_in_dim(visual_value_cache, key_block_offset, VISUAL_PER_CTX, 0).reshape(VISUAL_PER_CTX, KEY_VALUE_HEADS, HEAD_SIZE)
        key_wide = jnp.repeat(key_tile_rows, query_group_count, axis=1).astype(jnp.float32)
        value_wide = jnp.repeat(value_tile_rows, query_group_count, axis=1).astype(jnp.float32)
        segments = lax.dynamic_slice_in_dim(block_mask, (shard * (VISUAL_PER_CTX // SEG)).astype(jnp.int32), VISUAL_PER_CTX // SEG, 1)
        positions = key_block_offset + jnp.arange(VISUAL_PER_CTX, dtype=jnp.int32)
        allowed = (jnp.repeat(segments, SEG, axis=1) == 1) & (positions[None, :] < lengths[:, None])
        scores = jnp.einsum('rhd,khd->hrk', normed_wide, key_wide) * score_scale
        scores = jnp.where(allowed[None], scores, jnp.float32(-1e+30))
        block_max = lax.optimization_barrier(jnp.max(scores, axis=-1))
        weights = jnp.where(allowed[None], jnp.exp(scores - block_max[..., None]), jnp.float32(0.0))
        block_total = lax.optimization_barrier(jnp.sum(weights, axis=-1))
        block_num = jnp.einsum('hrk,khd->hrd', weights.astype(jnp.bfloat16).astype(jnp.float32), value_wide)
        old_num, old_max, old_total = state_carry
        highest = jnp.maximum(old_max, block_max)
        old_factor = jnp.exp(old_max - highest)
        new_factor = jnp.exp(block_max - highest)
        merged = (old_num * old_factor[..., None] + block_num * new_factor[..., None], highest, old_total * old_factor + block_total * new_factor)
        return (merged, None)
    start_state = (jnp.zeros((QUERY_HEAD_COUNT, TEXT, HEAD_SIZE), jnp.float32), jnp.full((QUERY_HEAD_COUNT, TEXT), -1e+30, jnp.float32), jnp.zeros((QUERY_HEAD_COUNT, TEXT), jnp.float32))
    final_state, unused = lax.scan(shard_step, start_state, jnp.arange(N_CTX, dtype=jnp.int32))
    numerator, row_max, total = final_state
    attended = (numerator / total[..., None]).astype(jnp.bfloat16)
    attended = jnp.transpose(attended, (1, 0, 2)).reshape(TEXT, QUERY_HEAD_COUNT * HEAD_SIZE)
    projected = jnp.dot(attended, o_weight, preferred_element_type=jnp.float32)
    return (text_states.astype(jnp.float32) + projected).astype(jnp.bfloat16)
```

```python
import functools

import jax
import jax.numpy as jnp
from jax import lax
from jax.experimental import pallas as pl
from jax.experimental.pallas import tpu as pltpu
from jax.sharding import PartitionSpec as P

MESH = pl.DeviceIdType.MESH
F32, BF16 = jnp.float32, jnp.bfloat16
HEAD = 128
HEADS = 4
WIDE = HEADS * HEAD
SIDE = 128
NEG = -1e30
FLOOR = -1e20
TINY = 1e-30
STEPS = 32000.0
LOG2E = 1.4426950408889634
PLANE = ((2, 3), (2, 2), (1, 3), (3, 3), (1, 2), (3, 2), (0, 3), (0, 2), (2, 1), (1, 1), (3, 1), (2, 0), (0, 1), (1, 0), (3, 0))
OUTER = ((1, 2), (1, 1), (1, 3), (1, 0), (0, 2), (0, 1), (0, 3))


def partner(v, i):
    return (v, v + 1 - 2 * (v % 2), (v + 2) % 4, 3 - v)[i]


def kernel(
    ts_hbm, qw_hbm, gain_hbm, keys, values, seen_hbm, length_hbm, ow_hbm, out,
    gain, seen, length, ts, qw, ow, q_mine, q_other, q_sib, q_part, q_in, q_rows, kb, vb, mark, marks, scores, part, part_in, att, att_sib, o_sum, o_part, o_in,
    swap_s, swap_r, rs1_s, rs1_r, kv_s, kv_r, fw_s, fw_r, ag1_s, ag1_r, rs2_s, rs2_r, ag2_s, ag2_r, c2_s, c2_r, rs3_s, rs3_r, load,
):
    ctx, head, tp = lax.axis_index("ctx"), lax.axis_index("head"), lax.axis_index("tp")
    x, z, c = ctx // 8, (ctx // 2) % 4, ctx % 2
    block = ctx // 2

    def chip(i, j):
        return partner(x, i) * 4 + partner(z, j)

    def on_plane(i, j):
        return (chip(i, j) * 2 + c, head, tp)

    sibling = (block * 2 + 1 - c, head, tp)

    def outer(i, j):
        return (head + i - 2 * i * head) * 4 + partner(tp, j)

    def on_outer(i, j):
        return (ctx, head + i - 2 * i * head, partner(tp, j))

    def copy(src, dst, sems, slot, device):
        return pltpu.make_async_remote_copy(
            src_ref=src, dst_ref=dst, send_sem=sems[0].at[slot], recv_sem=sems[1].at[slot], device_id=device, device_id_type=MESH
        )

    def rows(i, n):
        return pl.ds(pl.multiple_of(i * n, n), n)

    started = []

    def start(cp):
        cp.start()
        started.append(cp)
        return cp

    def arrived(cp):
        cp.wait_recv()

    def loaded(n):
        loads[n].wait()

    mine = pl.ds(pl.multiple_of(c * WIDE, WIDE), WIDE)
    other = pl.ds(pl.multiple_of((1 - c) * WIDE, WIDE), WIDE)
    loads = [
        pltpu.make_async_copy(ts_hbm, ts, load.at[0]),
        pltpu.make_async_copy(qw_hbm, qw, load.at[1]),
        pltpu.make_async_copy(keys, kb.at[0], load.at[2]),
        pltpu.make_async_copy(values, vb.at[0], load.at[3]),
        pltpu.make_async_copy(ow_hbm, ow, load.at[4]),
        pltpu.make_async_copy(gain_hbm, gain, load.at[5]),
        pltpu.make_async_copy(seen_hbm, seen, load.at[6]),
        pltpu.make_async_copy(length_hbm, length, load.at[7]),
    ]
    for cp in loads:
        cp.start()
    barrier = pltpu.get_barrier_semaphore()
    everyone = [on_plane(i, j) for i, j in PLANE] + [sibling] + [on_outer(i, j) for i, j in OUTER]
    for device in everyone:
        pl.semaphore_signal(barrier, inc=1, device_id=device, device_id_type=MESH)

    loaded(6)
    row = lax.broadcasted_iota(jnp.int32, (256, 256), 0)
    col = lax.broadcasted_iota(jnp.int32, (256, 256), 1)
    lane = lax.broadcasted_iota(jnp.int32, (256, SIDE), 1)
    flags = [jnp.sum(jnp.where(row == col, seen[n : n + 1, :].astype(F32), 0.0), axis=1, keepdims=True) for n in (0, 1)]
    mark[...] = jnp.where(lane == 0, flags[0], jnp.where(lane == 1, flags[1], 0.0)).astype(BF16)
    loaded(0)
    loaded(1)
    q_mine[...] = jnp.dot(ts[...], qw[:, mine], preferred_element_type=F32)
    q_other[...] = jnp.dot(ts[...], qw[:, other], preferred_element_type=F32)

    pl.semaphore_wait(barrier, len(everyone))

    halves = {}
    for i in (2, 1, 3, 0):
        part_rows = rows(partner(x, i), 64)
        halves[i] = start(copy(q_other.at[part_rows], q_sib.at[part_rows], (swap_s, swap_r), i, sibling))

    kv = {}

    bufs = ((keys, kb), (values, vb), (mark, marks))

    def of(ref, what, i):
        return ref.at[rows(partner(x, i), 64)] if what == 2 else ref

    def spread(what):
        src, dst = bufs[what]
        for i in (2, 1, 3) if what == 2 else (1, 3):
            kv[what, i] = start(copy(of(src, what, i), dst.at[2 * i], (kv_s, kv_r), 5 * what + i, on_plane(i, 0)))
        kv[what, 0] = start(copy(of(src, what, 0), dst.at[1], (fw_s, fw_r), 4 * what, sibling))

    def pass_on(what, partners):
        for i in partners:
            buf = bufs[what][1]
            for cp in (kv[what, i],) if (what, i) in kv else (kv[what, 4], kv[what, 5]):
                arrived(cp)
            kv[what, -i] = start(copy(buf.at[2 * i], buf.at[2 * i + 1], (fw_s, fw_r), 4 * what + i, sibling))

    def relay(what):
        buf = bufs[what][1]
        for n, i, lo in ((4, 3, 0), (5, 1, 256)):
            piece = pl.ds(lo, 256)
            kv[what, n] = start(copy(buf.at[2 * i, piece], buf.at[4, piece], (kv_s, kv_r), 5 * what + (0 if n == 4 else 4), on_plane(4 - i, 0)))

    spread(0)
    spread(2)

    rs1 = {}
    for i in (2, 1, 3, 0):
        arrived(halves[i])
        part_rows = rows(partner(x, i), 64)
        q = q_mine[part_rows, :] + q_sib[part_rows, :]
        power = jnp.ceil(jnp.log2(jnp.maximum(jnp.max(jnp.abs(q), axis=1, keepdims=True), TINY)))
        q_part[part_rows, :WIDE] = jnp.round(q * (STEPS * jnp.exp2(-power))).astype(jnp.int32).astype(jnp.int16)
        q_part[part_rows, WIDE:] = jnp.broadcast_to(power, (64, SIDE)).astype(jnp.int32).astype(jnp.int16)
        for j in (3, 2, 1, 0):
            if (i, j) != (0, 0):
                src = q_part.at[rows(chip(i, j), 16)]
                rs1[i, j] = start(copy(src, q_in.at[i * 4 + j], (rs1_s, rs1_r), i * 4 + j, on_plane(i, j)))
    spread(1)
    pass_on(0, (1, 3))
    relay(0)
    pass_on(1, (1, 3))
    relay(1)

    def decoded(coded):
        coded = coded.astype(jnp.int32).astype(F32)
        return coded[:, :WIDE] * (jnp.exp2(coded[:, WIDE : WIDE + 1]) / STEPS)

    q_own = decoded(q_part[rows(block, 16), :])
    for i, j in PLANE[::-1]:
        arrived(rs1[i, j])
        q_own = q_own + decoded(q_in[i * 4 + j])
    normed = []
    loaded(5)
    for n in range(HEADS):
        q = q_own[:, n * HEAD : (n + 1) * HEAD]
        mean_sq = jnp.mean(q * q, axis=-1, keepdims=True)
        normed.append((q * lax.rsqrt(mean_sq + 1e-05) * gain[...]).astype(BF16))
    q_rows[rows(z, 16), :] = jnp.concatenate(normed, axis=1)

    ag1 = [start(copy(q_rows.at[rows(z, 16)], q_rows.at[rows(z, 16)], (ag1_s, ag1_r), j, on_plane(0, j))) for j in (3, 2, 1)]

    pass_on(2, (1, 3, 2))
    pass_on(0, (2,))
    pass_on(1, (2,))

    loaded(7)
    row = lax.broadcasted_iota(jnp.int32, (64, 256), 0) + x * 64
    col = lax.broadcasted_iota(jnp.int32, (64, 256), 1)
    reach = jnp.sum(jnp.where(row == col, length[...].astype(F32), 0.0), axis=1, keepdims=True)
    token = lax.broadcasted_iota(jnp.int32, (64, 256), 1)

    for n in (2, 3, 4):
        loaded(n)
    for what in (0, 2):
        for i in (0, -2, -1, -3):
            arrived(kv[what, i])
    for cp in ag1:
        arrived(cp)
    q4 = jnp.concatenate([q_rows[:, n * HEAD : (n + 1) * HEAD] for n in range(HEADS)], axis=0)
    top = jnp.full((4 * 64, 128), NEG, F32)
    for slot in range(8):
        i, d = slot // 2, slot % 2
        k = kb[slot]
        flag = (mark[rows(x, 64), :] if slot == 0 else marks[slot]).astype(F32)
        s = lax.dot_general(q4, k, (((1,), (1,)), ((), ())), preferred_element_type=F32) * (LOG2E / HEAD**0.5)
        first = (chip(i, 0) * 2 + (c if d == 0 else 1 - c)) * 512
        ok = []
        for seg in range(2):
            limit = jnp.where(flag[:, seg : seg + 1] > 0.5, reach, 0.0) - (first + seg * 256).astype(F32)
            ok.append(token.astype(F32) < limit)
        ok = jnp.concatenate([jnp.where(o, 1.0, 0.0) for o in ok], axis=1) > 0.5
        s = jnp.where(ok[None], s.reshape(HEADS, 64, 512), NEG).reshape(HEADS * 64, 512)
        scores[:, slot * 512 : (slot + 1) * 512] = s
        for n in range(4):
            top = jnp.maximum(top, s[:, n * 128 : (n + 1) * 128])
    for i in (0, -2, -1, -3):
        arrived(kv[1, i])
    top = jnp.maximum(jnp.max(top, axis=1, keepdims=True), FLOOR)
    acc = jnp.zeros((HEADS * 64, 2 * HEAD), F32)
    ones = jnp.ones((512, HEAD), BF16)
    for slot in range(8):
        v = vb[slot]
        w = jnp.exp2(scores[:, slot * 512 : (slot + 1) * 512] - top).astype(BF16)
        acc = acc + jnp.dot(w, jnp.concatenate([v, ones], axis=1), preferred_element_type=F32)
    total = acc[:, HEAD:]
    some = total > 0.0
    safe = jnp.where(some, total, 1.0)
    local = acc[:, :HEAD] / safe
    lse = jnp.where(some, top + jnp.log2(safe), NEG)
    lane = lax.broadcasted_iota(jnp.int32, (64, SIDE), 1)
    side = jnp.zeros((64, SIDE), F32)
    for n in range(HEADS):
        part[:, n * HEAD : (n + 1) * HEAD] = local[n * 64 : (n + 1) * 64].astype(BF16)
        side = jnp.where((lane % 8 == n) & (lane < 24), lse[n * 64 : (n + 1) * 64], side)
    hi = side.astype(BF16).astype(F32)
    mid = (side - hi).astype(BF16).astype(F32)
    low = side - hi - mid
    part[:, WIDE:] = jnp.where(lane < 8, hi, jnp.where(lane < 16, mid, low)).astype(BF16)

    rs2 = [start(copy(part.at[rows(partner(z, j), 16)], part_in.at[j], (rs2_s, rs2_r), j, on_plane(0, j))) for j in (3, 2, 1)]
    for cp in rs2:
        arrived(cp)
    pieces = [part[rows(z, 16), :].astype(F32)] + [part_in[j].astype(F32) for j in (1, 2, 3)]
    lses = []
    for p in pieces:
        s = p[:, WIDE:]
        lses.append(s + pltpu.roll(s, SIDE - 8, 1) + pltpu.roll(s, SIDE - 16, 1))
    best = functools.reduce(jnp.maximum, lses)
    shares = [jnp.exp2(s - best) for s in lses]
    norm = functools.reduce(jnp.add, shares)
    shares = [s / norm for s in shares]
    merged = []
    for n in range(HEADS):
        terms = [s[:, n : n + 1] * p[:, n * HEAD : (n + 1) * HEAD] for s, p in zip(shares, pieces)]
        merged.append(functools.reduce(jnp.add, terms).astype(BF16))
    att[rows(block, 16), :] = jnp.concatenate(merged, axis=1)

    ag2 = [start(copy(att.at[rows(block, 16)], att.at[rows(block, 16)], (ag2_s, ag2_r), i * 4 + j, on_plane(i, j))) for i, j in PLANE]
    c2 = [start(copy(att.at[rows(block, 16)], att_sib.at[rows(block, 16)], (c2_s, c2_r), 0, sibling))]
    for cp, (i, j) in reversed(list(zip(ag2, PLANE))):
        arrived(cp)
        piece = rows(chip(i, j), 16)
        c2.append(start(copy(att.at[piece], att_sib.at[piece], (c2_s, c2_r), i * 4 + j, sibling)))
    o_sum[...] = jnp.dot(att[...], ow[mine, :], preferred_element_type=F32)
    for cp in c2:
        arrived(cp)
    o_all = o_sum[...] + jnp.dot(att_sib[...], ow[other, :], preferred_element_type=F32)
    o_sum[...] = o_all
    o_part[...] = o_all.astype(BF16)

    rs3 = [start(copy(o_part.at[rows(outer(i, j), 32)], o_in.at[i * 4 + j], (rs3_s, rs3_r), i * 4 + j, on_outer(i, j))) for i, j in OUTER]
    here = rows(head * 4 + tp, 32)
    result = ts[here, :].astype(F32) + o_sum[here, :]
    for cp, (i, j) in zip(rs3, OUTER):
        arrived(cp)
        result = result + o_in[i * 4 + j].astype(F32)
    out[...] = result.astype(BF16)
    for cp in started:
        cp.wait_send()


def shards(text_states, q_weight, q_gain, visual_key_cache, visual_value_cache, block_mask, lengths, o_weight):
    vmem = pl.BlockSpec(memory_space=pltpu.VMEM)
    hbm = pl.BlockSpec(memory_space=pltpu.HBM)
    dma = pltpu.SemaphoreType.DMA
    return pl.pallas_call(
        kernel,
        out_shape=jax.ShapeDtypeStruct((32, 256), BF16),
        in_specs=[hbm] * 8,
        out_specs=vmem,
        scratch_shapes=[
            pltpu.VMEM((1, HEAD), F32),
            pltpu.VMEM((2, 256), jnp.int32),
            pltpu.VMEM((1, 256), jnp.int32),
            pltpu.VMEM((256, 256), BF16),
            pltpu.VMEM((256, 2 * WIDE), BF16),
            pltpu.VMEM((2 * WIDE, 256), BF16),
            pltpu.VMEM((256, WIDE), F32),
            pltpu.VMEM((256, WIDE), F32),
            pltpu.VMEM((256, WIDE), F32),
            pltpu.VMEM((256, WIDE + SIDE), jnp.int16),
            pltpu.VMEM((16, 16, WIDE + SIDE), jnp.int16),
            pltpu.VMEM((64, WIDE), BF16),
            pltpu.VMEM((8, 512, HEAD), BF16),
            pltpu.VMEM((8, 512, HEAD), BF16),
            pltpu.VMEM((256, SIDE), BF16),
            pltpu.VMEM((8, 64, SIDE), BF16),
            pltpu.VMEM((HEADS * 64, 4096), F32),
            pltpu.VMEM((64, WIDE + SIDE), BF16),
            pltpu.VMEM((4, 16, WIDE + SIDE), BF16),
            pltpu.VMEM((256, WIDE), BF16),
            pltpu.VMEM((256, WIDE), BF16),
            pltpu.VMEM((256, 256), F32),
            pltpu.VMEM((256, 256), BF16),
            pltpu.VMEM((8, 32, 256), BF16),
            dma((4,)), dma((4,)),
            dma((16,)), dma((16,)),
            dma((15,)), dma((15,)),
            dma((12,)), dma((12,)),
            dma((4,)), dma((4,)),
            dma((4,)), dma((4,)),
            dma((16,)), dma((16,)),
            dma((16,)), dma((16,)),
            dma((8,)), dma((8,)),
            dma((8,)),
        ],
        compiler_params=pltpu.CompilerParams(collective_id=0, has_side_effects=True, vmem_limit_bytes=60 * 1024 * 1024),
    )(text_states, q_weight, q_gain.reshape(1, HEAD), visual_key_cache, visual_value_cache, block_mask.T, lengths.reshape(1, 256), o_weight)


def solution(mesh):
    in_specs = (
        P(None, "ctx"),
        P("ctx", ("head", "tp")),
        P(),
        P("ctx", ("head", "tp")),
        P("ctx", ("head", "tp")),
        P(None, "ctx"),
        P(),
        P(("head", "tp"), "ctx"),
    )
    out_specs = P(("head", "tp"), "ctx")
    return jax.shard_map(shards, mesh=mesh, in_specs=in_specs, out_specs=out_specs, check_vma=False)
```

```python
import functools

import jax
import jax.numpy as jnp
from jax import lax
from jax.experimental import pallas as pl
from jax.experimental.pallas import tpu as pltpu
from jax.sharding import PartitionSpec as P

MESH = pl.DeviceIdType.MESH
F32, BF16 = jnp.float32, jnp.bfloat16
HEAD = 128
HEADS = 4
WIDE = HEADS * HEAD
SIDE = 128
NEG = -1e30
FLOOR = -1e20
TINY = 1e-30
STEPS = 32000.0
LOG2E = 1.4426950408889634
PLANE = ((2, 3), (2, 2), (1, 3), (3, 3), (1, 2), (3, 2), (0, 3), (0, 2), (2, 1), (1, 1), (3, 1), (2, 0), (0, 1), (1, 0), (3, 0))
OUTER = ((1, 2), (1, 1), (1, 3), (1, 0), (0, 2), (0, 1), (0, 3))


def partner(v, i):
    return (v, v + 1 - 2 * (v % 2), (v + 2) % 4, 3 - v)[i]


def kernel(
    ts_hbm, qw_hbm, gain_hbm, keys, values, seen_hbm, length_hbm, ow_hbm, out,
    gain, seen, length, ts, qw, ow, q_mine, q_other, q_sib, q_part, q_pow, q_in, pow_in, q_rows, kb, vb, mark, marks, scores, part, part_in, att, att_sib, o_sum, o_part, o_in,
    swap_s, swap_r, rs1_s, rs1_r, kv_s, kv_r, fw_s, fw_r, ag1_s, ag1_r, rs2_s, rs2_r, ag2_s, ag2_r, c2_s, c2_r, rs3_s, rs3_r, load,
):
    ctx, head, tp = lax.axis_index("ctx"), lax.axis_index("head"), lax.axis_index("tp")
    x, z, c = ctx // 8, (ctx // 2) % 4, ctx % 2
    block = ctx // 2

    def chip(i, j):
        return partner(x, i) * 4 + partner(z, j)

    def on_plane(i, j):
        return (chip(i, j) * 2 + c, head, tp)

    sibling = (block * 2 + 1 - c, head, tp)

    def outer(i, j):
        return (head + i - 2 * i * head) * 4 + partner(tp, j)

    def on_outer(i, j):
        return (ctx, head + i - 2 * i * head, partner(tp, j))

    def copy(src, dst, sems, slot, device):
        return pltpu.make_async_remote_copy(
            src_ref=src, dst_ref=dst, send_sem=sems[0].at[slot], recv_sem=sems[1].at[slot], device_id=device, device_id_type=MESH
        )

    def rows(i, n):
        return pl.ds(pl.multiple_of(i * n, n), n)

    started = []

    def start(cp):
        cp.start()
        started.append(cp)
        return cp

    def arrived(cp):
        cp.wait_recv()

    def loaded(n):
        loads[n].wait()

    mine = pl.ds(pl.multiple_of(c * WIDE, WIDE), WIDE)
    other = pl.ds(pl.multiple_of((1 - c) * WIDE, WIDE), WIDE)
    loads = [
        pltpu.make_async_copy(ts_hbm, ts, load.at[0]),
        pltpu.make_async_copy(qw_hbm, qw, load.at[1]),
        pltpu.make_async_copy(keys, kb.at[0], load.at[2]),
        pltpu.make_async_copy(values, vb.at[0], load.at[3]),
        pltpu.make_async_copy(ow_hbm, ow, load.at[4]),
        pltpu.make_async_copy(gain_hbm, gain, load.at[5]),
        pltpu.make_async_copy(seen_hbm, seen, load.at[6]),
        pltpu.make_async_copy(length_hbm, length, load.at[7]),
    ]
    for cp in loads:
        cp.start()
    barrier = pltpu.get_barrier_semaphore()
    everyone = [on_plane(i, j) for i, j in PLANE] + [sibling] + [on_outer(i, j) for i, j in OUTER]
    for device in everyone:
        pl.semaphore_signal(barrier, inc=1, device_id=device, device_id_type=MESH)

    loaded(6)
    row = lax.broadcasted_iota(jnp.int32, (256, 256), 0)
    col = lax.broadcasted_iota(jnp.int32, (256, 256), 1)
    lane = lax.broadcasted_iota(jnp.int32, (256, SIDE), 1)
    flags = [jnp.sum(jnp.where(row == col, seen[n : n + 1, :].astype(F32), 0.0), axis=1, keepdims=True) for n in (0, 1)]
    mark[...] = jnp.where(lane == 0, flags[0], jnp.where(lane == 1, flags[1], 0.0)).astype(BF16)
    loaded(0)
    loaded(1)
    q_mine[...] = jnp.dot(ts[...], qw[:, mine], preferred_element_type=F32)
    q_other[...] = jnp.dot(ts[...], qw[:, other], preferred_element_type=F32)

    pl.semaphore_wait(barrier, len(everyone))

    halves = {}
    for i in (2, 1, 3, 0):
        part_rows = rows(partner(x, i), 64)
        halves[i] = start(copy(q_other.at[part_rows], q_sib.at[part_rows], (swap_s, swap_r), i, sibling))

    kv = {}

    bufs = ((keys, kb), (values, vb), (mark, marks))

    def of(ref, what, i):
        return ref.at[rows(partner(x, i), 64)] if what == 2 else ref

    def spread(what):
        src, dst = bufs[what]
        for i in (2, 1, 3) if what == 2 else (1, 3):
            kv[what, i] = start(copy(of(src, what, i), dst.at[2 * i], (kv_s, kv_r), 5 * what + i, on_plane(i, 0)))
        kv[what, 0] = start(copy(of(src, what, 0), dst.at[1], (fw_s, fw_r), 4 * what, sibling))

    def pass_on(what, partners):
        for i in partners:
            buf = bufs[what][1]
            for cp in (kv[what, i],) if (what, i) in kv else (kv[what, 4], kv[what, 5]):
                arrived(cp)
            kv[what, -i] = start(copy(buf.at[2 * i], buf.at[2 * i + 1], (fw_s, fw_r), 4 * what + i, sibling))

    def relay(what):
        buf = bufs[what][1]
        for n, i, lo in ((4, 3, 0), (5, 1, 256)):
            piece = pl.ds(lo, 256)
            kv[what, n] = start(copy(buf.at[2 * i, piece], buf.at[4, piece], (kv_s, kv_r), 5 * what + (0 if n == 4 else 4), on_plane(4 - i, 0)))

    spread(0)
    spread(2)

    diagonal = lax.broadcasted_iota(jnp.int32, (16, 128), 0) == lax.broadcasted_iota(jnp.int32, (16, 128), 1)

    rs1 = {}
    for i in (2, 1, 3, 0):
        arrived(halves[i])
        part_rows = rows(partner(x, i), 64)
        q = q_mine[part_rows, :] + q_sib[part_rows, :]
        power = jnp.ceil(jnp.log2(jnp.maximum(jnp.max(jnp.abs(q), axis=1, keepdims=True), TINY)))
        q_part[part_rows, :] = jnp.round(q * (STEPS * jnp.exp2(-power))).astype(jnp.int32).astype(jnp.int16)
        for n in range(4):
            laid = jnp.where(diagonal, power[16 * n : 16 * n + 16], 0.0)
            q_pow[partner(x, i) * 4 + n] = jnp.sum(laid, axis=0, keepdims=True)
        for j in (3, 2, 1, 0):
            if (i, j) != (0, 0):
                src = q_part.at[rows(chip(i, j), 16)]
                rs1[i, j] = start(copy(src, q_in.at[i * 4 + j], (rs1_s, rs1_r), i * 4 + j, on_plane(i, j)))
                src = q_pow.at[chip(i, j)]
                rs1[j, i, 1] = start(copy(src, pow_in.at[i * 4 + j], (rs1_s, rs1_r), 16 + i * 4 + j, on_plane(i, j)))
    spread(1)
    pass_on(0, (1, 3))
    relay(0)
    pass_on(1, (1, 3))
    relay(1)

    def decoded(coded, powers):
        power = jnp.sum(jnp.where(diagonal, powers, 0.0), axis=1, keepdims=True)
        return coded.astype(jnp.int32).astype(F32) * (jnp.exp2(power) / STEPS)

    q_own = decoded(q_part[rows(block, 16), :], q_pow[block])
    for i, j in PLANE[::-1]:
        arrived(rs1[i, j])
        arrived(rs1[j, i, 1])
        q_own = q_own + decoded(q_in[i * 4 + j], pow_in[i * 4 + j])
    normed = []
    loaded(5)
    for n in range(HEADS):
        q = q_own[:, n * HEAD : (n + 1) * HEAD]
        mean_sq = jnp.mean(q * q, axis=-1, keepdims=True)
        normed.append((q * lax.rsqrt(mean_sq + 1e-05) * gain[...]).astype(BF16))
    q_rows[rows(z, 16), :] = jnp.concatenate(normed, axis=1)

    ag1 = [start(copy(q_rows.at[rows(z, 16)], q_rows.at[rows(z, 16)], (ag1_s, ag1_r), j, on_plane(0, j))) for j in (3, 2, 1)]

    pass_on(2, (1, 3, 2))
    pass_on(0, (2,))
    pass_on(1, (2,))

    loaded(7)
    row = lax.broadcasted_iota(jnp.int32, (64, 256), 0) + x * 64
    col = lax.broadcasted_iota(jnp.int32, (64, 256), 1)
    reach = jnp.sum(jnp.where(row == col, length[...].astype(F32), 0.0), axis=1, keepdims=True)
    token = lax.broadcasted_iota(jnp.int32, (64, 256), 1)

    for n in (2, 3, 4):
        loaded(n)
    for what in (0, 2):
        for i in (0, -2, -1, -3):
            arrived(kv[what, i])
    for cp in ag1:
        arrived(cp)
    q4 = jnp.concatenate([q_rows[:, n * HEAD : (n + 1) * HEAD] for n in range(HEADS)], axis=0)
    top = jnp.full((4 * 64, 128), NEG, F32)
    for slot in range(8):
        i, d = slot // 2, slot % 2
        k = kb[slot]
        flag = (mark[rows(x, 64), :] if slot == 0 else marks[slot]).astype(F32)
        s = lax.dot_general(q4, k, (((1,), (1,)), ((), ())), preferred_element_type=F32) * (LOG2E / HEAD**0.5)
        first = (chip(i, 0) * 2 + (c if d == 0 else 1 - c)) * 512
        ok = []
        for seg in range(2):
            limit = jnp.where(flag[:, seg : seg + 1] > 0.5, reach, 0.0) - (first + seg * 256).astype(F32)
            ok.append(token.astype(F32) < limit)
        ok = jnp.concatenate([jnp.where(o, 1.0, 0.0) for o in ok], axis=1) > 0.5
        s = jnp.where(ok[None], s.reshape(HEADS, 64, 512), NEG).reshape(HEADS * 64, 512)
        scores[:, slot * 512 : (slot + 1) * 512] = s
        for n in range(4):
            top = jnp.maximum(top, s[:, n * 128 : (n + 1) * 128])
    for i in (0, -2, -1, -3):
        arrived(kv[1, i])
    top = jnp.maximum(jnp.max(top, axis=1, keepdims=True), FLOOR)
    ones = jnp.ones((512, HEAD), BF16)
    lane = lax.broadcasted_iota(jnp.int32, (64, SIDE), 1)
    rs2 = {}
    for g in range(2):
        mid_rows = slice(g * 128, (g + 1) * 128)
        acc = jnp.zeros((128, 2 * HEAD), F32)
        for slot in range(8):
            w = jnp.exp2(scores[mid_rows, slot * 512 : (slot + 1) * 512] - top[mid_rows]).astype(BF16)
            acc = acc + jnp.dot(w, jnp.concatenate([vb[slot], ones], axis=1), preferred_element_type=F32)
        total = acc[:, HEAD:]
        some = total > 0.0
        safe = jnp.where(some, total, 1.0)
        local = acc[:, :HEAD] / safe
        lse = jnp.where(some, top[mid_rows] + jnp.log2(safe), NEG)
        side = jnp.zeros((64, SIDE), F32)
        for n in range(2):
            part[g, :, n * HEAD : (n + 1) * HEAD] = local[n * 64 : (n + 1) * 64].astype(BF16)
            side = jnp.where((lane % 8 == n) & (lane < 24), lse[n * 64 : (n + 1) * 64], side)
        hi = side.astype(BF16).astype(F32)
        mid = (side - hi).astype(BF16).astype(F32)
        low = side - hi - mid
        part[g, :, 2 * HEAD :] = jnp.where(lane < 8, hi, jnp.where(lane < 16, mid, low)).astype(BF16)
        for j in (3, 2, 1):
            src = part.at[g, rows(partner(z, j), 16)]
            rs2[g, j] = start(copy(src, part_in.at[g, j], (rs2_s, rs2_r), 4 * g + j, on_plane(0, j)))

    ag2 = {}
    for g in range(2):
        for j in (1, 2, 3):
            arrived(rs2[g, j])
        pieces = [part[g, rows(z, 16), :].astype(F32)] + [part_in[g, j].astype(F32) for j in (1, 2, 3)]
        lses = []
        for p in pieces:
            s = p[:, 2 * HEAD :]
            lses.append(s + pltpu.roll(s, SIDE - 8, 1) + pltpu.roll(s, SIDE - 16, 1))
        best = functools.reduce(jnp.maximum, lses)
        shares = [jnp.exp2(s - best) for s in lses]
        norm = functools.reduce(jnp.add, shares)
        shares = [s / norm for s in shares]
        merged = []
        for n in range(2):
            terms = [s[:, n : n + 1] * p[:, n * HEAD : (n + 1) * HEAD] for s, p in zip(shares, pieces)]
            merged.append(functools.reduce(jnp.add, terms).astype(BF16))
        att[g, rows(block, 16), :] = jnp.concatenate(merged, axis=1)
        for i, j in PLANE:
            piece = att.at[g, rows(block, 16)]
            ag2[g, i, j] = start(copy(piece, piece, (ag2_s, ag2_r), 16 * g + i * 4 + j, on_plane(i, j)))

    def weights(core, g):
        return ow[pl.ds(pl.multiple_of(core * WIDE + g * 256, 256), 256), :]

    c2 = []
    for g in range(2):
        for i, j in PLANE[::-1]:
            arrived(ag2[g, i, j])
        c2.append(start(copy(att.at[g], att_sib.at[g], (c2_s, c2_r), g, sibling)))
        if g == 0:
            o_sum[...] = jnp.dot(att[0], weights(c, 0), preferred_element_type=F32)
    arrived(c2[0])
    o_sum[...] += jnp.dot(att[1], weights(c, 1), preferred_element_type=F32) + jnp.dot(att_sib[0], weights(1 - c, 0), preferred_element_type=F32)
    arrived(c2[1])
    o_all = o_sum[...] + jnp.dot(att_sib[1], weights(1 - c, 1), preferred_element_type=F32)
    o_sum[...] = o_all
    o_part[...] = o_all.astype(BF16)
    rs3 = {}
    for i, j in OUTER:
        rs3[i, j] = start(copy(o_part.at[rows(outer(i, j), 32)], o_in.at[i * 4 + j], (rs3_s, rs3_r), i * 4 + j, on_outer(i, j)))
    here = rows(head * 4 + tp, 32)
    result = ts[here, :].astype(F32) + o_sum[here, :]
    for i, j in OUTER[::-1]:
        arrived(rs3[i, j])
        result = result + o_in[i * 4 + j].astype(F32)
    out[...] = result.astype(BF16)
    for cp in started:
        cp.wait_send()


def shards(text_states, q_weight, q_gain, visual_key_cache, visual_value_cache, block_mask, lengths, o_weight):
    vmem = pl.BlockSpec(memory_space=pltpu.VMEM)
    hbm = pl.BlockSpec(memory_space=pltpu.HBM)
    dma = pltpu.SemaphoreType.DMA
    return pl.pallas_call(
        kernel,
        out_shape=jax.ShapeDtypeStruct((32, 256), BF16),
        in_specs=[hbm] * 8,
        out_specs=vmem,
        scratch_shapes=[
            pltpu.VMEM((1, HEAD), F32),
            pltpu.VMEM((2, 256), jnp.int32),
            pltpu.VMEM((1, 256), jnp.int32),
            pltpu.VMEM((256, 256), BF16),
            pltpu.VMEM((256, 2 * WIDE), BF16),
            pltpu.VMEM((2 * WIDE, 256), BF16),
            pltpu.VMEM((256, WIDE), F32),
            pltpu.VMEM((256, WIDE), F32),
            pltpu.VMEM((256, WIDE), F32),
            pltpu.VMEM((256, WIDE), jnp.int16),
            pltpu.VMEM((16, 1, 128), F32),
            pltpu.VMEM((16, 16, WIDE), jnp.int16),
            pltpu.VMEM((16, 1, 128), F32),
            pltpu.VMEM((64, WIDE), BF16),
            pltpu.VMEM((8, 512, HEAD), BF16),
            pltpu.VMEM((8, 512, HEAD), BF16),
            pltpu.VMEM((256, SIDE), BF16),
            pltpu.VMEM((8, 64, SIDE), BF16),
            pltpu.VMEM((HEADS * 64, 4096), F32),
            pltpu.VMEM((2, 64, 2 * HEAD + SIDE), BF16),
            pltpu.VMEM((2, 4, 16, 2 * HEAD + SIDE), BF16),
            pltpu.VMEM((2, 256, 2 * HEAD), BF16),
            pltpu.VMEM((2, 256, 2 * HEAD), BF16),
            pltpu.VMEM((256, 256), F32),
            pltpu.VMEM((256, 256), BF16),
            pltpu.VMEM((8, 32, 256), BF16),
            dma((4,)), dma((4,)),
            dma((32,)), dma((32,)),
            dma((15,)), dma((15,)),
            dma((12,)), dma((12,)),
            dma((4,)), dma((4,)),
            dma((8,)), dma((8,)),
            dma((32,)), dma((32,)),
            dma((2,)), dma((2,)),
            dma((8,)), dma((8,)),
            dma((8,)),
        ],
        compiler_params=pltpu.CompilerParams(collective_id=0, has_side_effects=True, vmem_limit_bytes=40 * 1024 * 1024),
    )(*[pltpu.with_memory_space_constraint(a, pltpu.HBM) for a in (text_states, q_weight, q_gain.reshape(1, HEAD), visual_key_cache, visual_value_cache, block_mask.T, lengths.reshape(1, 256), o_weight)])


def solution(mesh):
    in_specs = (
        P(None, "ctx"),
        P("ctx", ("head", "tp")),
        P(),
        P("ctx", ("head", "tp")),
        P("ctx", ("head", "tp")),
        P(None, "ctx"),
        P(),
        P(("head", "tp"), "ctx"),
    )
    out_specs = P(("head", "tp"), "ctx")
    return jax.shard_map(shards, mesh=mesh, in_specs=in_specs, out_specs=out_specs, check_vma=False)
```

```python
import functools

import jax
import jax.numpy as jnp
from jax import lax
from jax.experimental import pallas as pl
from jax.experimental.pallas import tpu as pltpu
from jax.sharding import PartitionSpec as P

MESH = pl.DeviceIdType.MESH
F32, BF16 = jnp.float32, jnp.bfloat16
HEAD = 128
HEADS = 4
WIDE = HEADS * HEAD
SIDE = 128
NEG = -1e30
FLOOR = -1e20
TINY = 1e-30
STEPS = 32000.0
LOG2E = 1.4426950408889634
PLANE = ((2, 3), (2, 2), (1, 3), (3, 3), (1, 2), (3, 2), (0, 3), (0, 2), (2, 1), (1, 1), (3, 1), (2, 0), (0, 1), (1, 0), (3, 0))
OUTER = ((1, 2), (1, 1), (1, 3), (1, 0), (0, 2), (0, 1), (0, 3))


def partner(v, i):
    return (v, v + 1 - 2 * (v % 2), (v + 2) % 4, 3 - v)[i]


def kernel(
    ts_hbm, qw_hbm, gain_hbm, keys, values, seen_hbm, length_hbm, ow_hbm, out,
    gain, seen, length, ts, qw, ow, q_mine, q_other, q_sib, q_part, q_pow, q_in, pow_in, q_rows, kb, vb, mark, marks, scores, part, part_in, att, att_sib, o_sum, o_part, o_in,
    swap_s, swap_r, rs1_s, rs1_r, kv_s, kv_r, fw_s, fw_r, ag1_s, ag1_r, rs2_s, rs2_r, ag2_s, ag2_r, c2_s, c2_r, rs3_s, rs3_r, load,
):
    ctx, head, tp = lax.axis_index("ctx"), lax.axis_index("head"), lax.axis_index("tp")
    x, z, c = ctx // 8, (ctx // 2) % 4, ctx % 2
    block = ctx // 2

    def chip(i, j):
        return partner(x, i) * 4 + partner(z, j)

    def on_plane(i, j):
        return (chip(i, j) * 2 + c, head, tp)

    sibling = (block * 2 + 1 - c, head, tp)

    def outer(i, j):
        return (head + i - 2 * i * head) * 4 + partner(tp, j)

    def on_outer(i, j):
        return (ctx, head + i - 2 * i * head, partner(tp, j))

    def copy(src, dst, sems, slot, device):
        return pltpu.make_async_remote_copy(
            src_ref=src, dst_ref=dst, send_sem=sems[0].at[slot], recv_sem=sems[1].at[slot], device_id=device, device_id_type=MESH
        )

    def rows(i, n):
        return pl.ds(pl.multiple_of(i * n, n), n)

    started = []

    def start(cp):
        cp.start()
        started.append(cp)
        return cp

    def arrived(cp):
        cp.wait_recv()

    def loaded(n):
        loads[n].wait()

    barrier = pltpu.get_barrier_semaphore()
    everyone = [on_outer(i, j) for i, j in OUTER] + [on_plane(i, j) for i, j in PLANE] + [sibling]
    for device in everyone:
        pl.semaphore_signal(barrier, inc=1, device_id=device, device_id_type=MESH)

    mine = pl.ds(pl.multiple_of(c * WIDE, WIDE), WIDE)
    other = pl.ds(pl.multiple_of((1 - c) * WIDE, WIDE), WIDE)
    loads = [
        pltpu.make_async_copy(ts_hbm, ts, load.at[0]),
        pltpu.make_async_copy(qw_hbm, qw, load.at[1]),
        pltpu.make_async_copy(keys, kb.at[0], load.at[2]),
        pltpu.make_async_copy(values, vb.at[0], load.at[3]),
        pltpu.make_async_copy(ow_hbm, ow, load.at[4]),
        pltpu.make_async_copy(gain_hbm, gain, load.at[5]),
        pltpu.make_async_copy(seen_hbm, seen, load.at[6]),
        pltpu.make_async_copy(length_hbm, length, load.at[7]),
    ]
    for cp in loads:
        cp.start()
    loaded(6)
    row = lax.broadcasted_iota(jnp.int32, (256, 256), 0)
    col = lax.broadcasted_iota(jnp.int32, (256, 256), 1)
    lane = lax.broadcasted_iota(jnp.int32, (256, SIDE), 1)
    flags = [jnp.sum(jnp.where(row == col, seen[n : n + 1, :].astype(F32), 0.0), axis=1, keepdims=True) for n in (0, 1)]
    mark[...] = jnp.where(lane == 0, flags[0], jnp.where(lane == 1, flags[1], 0.0)).astype(BF16)
    loaded(0)
    loaded(1)
    q_mine[...] = jnp.dot(ts[...], qw[:, mine], preferred_element_type=F32)
    q_other[...] = jnp.dot(ts[...], qw[:, other], preferred_element_type=F32)

    pl.semaphore_wait(barrier, len(everyone))

    halves = {}
    for i in (0, 2, 1, 3):
        part_rows = rows(partner(x, i), 64)
        halves[i] = start(copy(q_other.at[part_rows], q_sib.at[part_rows], (swap_s, swap_r), i, sibling))

    kv = {}

    bufs = ((keys, kb), (values, vb), (mark, marks))

    def of(ref, what, i):
        return ref.at[rows(partner(x, i), 64)] if what == 2 else ref

    def spread(what):
        src, dst = bufs[what]
        for i in (2, 1, 3) if what == 2 else (1, 3):
            kv[what, i] = start(copy(of(src, what, i), dst.at[2 * i], (kv_s, kv_r), 5 * what + i, on_plane(i, 0)))
        kv[what, 0] = start(copy(of(src, what, 0), dst.at[1], (fw_s, fw_r), 4 * what, sibling))

    def pass_on(what, partners):
        for i in partners:
            buf = bufs[what][1]
            for cp in (kv[what, i],) if (what, i) in kv else (kv[what, 4], kv[what, 5]):
                arrived(cp)
            kv[what, -i] = start(copy(buf.at[2 * i], buf.at[2 * i + 1], (fw_s, fw_r), 4 * what + i, sibling))

    def relay(what):
        buf = bufs[what][1]
        for n, i, lo in ((4, 3, 0), (5, 1, 256)):
            piece = pl.ds(lo, 256)
            kv[what, n] = start(copy(buf.at[2 * i, piece], buf.at[4, piece], (kv_s, kv_r), 5 * what + (0 if n == 4 else 4), on_plane(4 - i, 0)))

    spread(0)
    spread(2)

    diagonal = lax.broadcasted_iota(jnp.int32, (16, 128), 0) == lax.broadcasted_iota(jnp.int32, (16, 128), 1)

    rs1 = {}
    for i in (0, 2, 1, 3):
        arrived(halves[i])
        part_rows = rows(partner(x, i), 64)
        q = q_mine[part_rows, :] + q_sib[part_rows, :]
        power = jnp.ceil(jnp.log2(jnp.maximum(jnp.max(jnp.abs(q), axis=1, keepdims=True), TINY)))
        q_part[part_rows, :] = jnp.round(q * (STEPS * jnp.exp2(-power))).astype(jnp.int32).astype(jnp.int16)
        for n in range(4):
            laid = jnp.where(diagonal, power[16 * n : 16 * n + 16], 0.0)
            q_pow[partner(x, i) * 4 + n] = jnp.sum(laid, axis=0, keepdims=True)
        for j in (3, 2, 1, 0):
            if (i, j) != (0, 0):
                src = q_part.at[rows(chip(i, j), 16)]
                rs1[i, j] = start(copy(src, q_in.at[i * 4 + j], (rs1_s, rs1_r), i * 4 + j, on_plane(i, j)))
                src = q_pow.at[chip(i, j)]
                rs1[j, i, 1] = start(copy(src, pow_in.at[i * 4 + j], (rs1_s, rs1_r), 16 + i * 4 + j, on_plane(i, j)))
    spread(1)
    pass_on(0, (1, 3))
    relay(0)

    def decoded(coded, powers):
        power = jnp.sum(jnp.where(diagonal, powers, 0.0), axis=1, keepdims=True)
        return coded.astype(jnp.int32).astype(F32) * (jnp.exp2(power) / STEPS)

    q_own = decoded(q_part[rows(block, 16), :], q_pow[block])
    for i, j in PLANE[::-1]:
        arrived(rs1[i, j])
        arrived(rs1[j, i, 1])
        q_own = q_own + decoded(q_in[i * 4 + j], pow_in[i * 4 + j])
    normed = []
    loaded(5)
    for n in range(HEADS):
        q = q_own[:, n * HEAD : (n + 1) * HEAD]
        mean_sq = jnp.mean(q * q, axis=-1, keepdims=True)
        normed.append((q * lax.rsqrt(mean_sq + 1e-05) * gain[...]).astype(BF16))
    q_rows[rows(z, 16), :] = jnp.concatenate(normed, axis=1)

    ag1 = [start(copy(q_rows.at[rows(z, 16)], q_rows.at[rows(z, 16)], (ag1_s, ag1_r), j, on_plane(0, j))) for j in (3, 2, 1)]

    pass_on(1, (1, 3))
    relay(1)
    pass_on(2, (1, 3, 2))
    pass_on(0, (2,))

    loaded(7)
    row = lax.broadcasted_iota(jnp.int32, (64, 256), 0) + x * 64
    col = lax.broadcasted_iota(jnp.int32, (64, 256), 1)
    reach = jnp.sum(jnp.where(row == col, length[...].astype(F32), 0.0), axis=1, keepdims=True)
    token = lax.broadcasted_iota(jnp.int32, (64, 256), 1)

    for n in (2, 3, 4):
        loaded(n)
    for what in (0, 2):
        for i in (0, -2, -1, -3):
            arrived(kv[what, i])
    for cp in ag1:
        arrived(cp)
    token_f = token.astype(F32)
    q4 = jnp.concatenate([q_rows[:, n * HEAD : (n + 1) * HEAD] for n in range(HEADS)], axis=0)
    top = jnp.full((4 * 64, 128), NEG, F32)
    for slot in range(8):
        i, d = slot // 2, slot % 2
        k = kb[slot]
        flag = (mark[rows(x, 64), :] if slot == 0 else marks[slot]).astype(F32)
        s = lax.dot_general(q4, k, (((1,), (1,)), ((), ())), preferred_element_type=F32) * (LOG2E / HEAD**0.5)
        first = (chip(i, 0) * 2 + (c if d == 0 else 1 - c)) * 512
        for seg in range(2):
            limit = jnp.where(flag[:, seg : seg + 1] > 0.5, reach, 0.0) - (first + seg * 256).astype(F32)
            ok = token_f < limit
            allowed = jnp.where(ok[None], s[:, seg * 256 : (seg + 1) * 256].reshape(HEADS, 64, 256), NEG).reshape(HEADS * 64, 256)
            scores[:, slot * 512 + seg * 256 : slot * 512 + (seg + 1) * 256] = allowed
            top = jnp.maximum(top, jnp.maximum(allowed[:, :128], allowed[:, 128:]))
    pass_on(1, (2,))
    for i in (0, -1, -3):
        arrived(kv[1, i])
    top = jnp.maximum(jnp.max(top, axis=1, keepdims=True), FLOOR)
    ones = jnp.ones((512, HEAD), BF16)
    lane = lax.broadcasted_iota(jnp.int32, (64, SIDE), 1)
    rs2 = {}
    for g in range(2):
        mid_rows = slice(g * 128, (g + 1) * 128)
        acc = jnp.zeros((128, 2 * HEAD), F32)
        for slot in (0, 1, 2, 6, 3, 7, 5, 4):
            if g == 0 and slot == 5:
                arrived(kv[1, -2])
            w = jnp.exp2(scores[mid_rows, slot * 512 : (slot + 1) * 512] - top[mid_rows]).astype(BF16)
            acc = acc + jnp.dot(w, jnp.concatenate([vb[slot], ones], axis=1), preferred_element_type=F32)
        total = acc[:, HEAD:]
        some = total > 0.0
        safe = jnp.where(some, total, 1.0)
        local = acc[:, :HEAD] / safe
        lse = jnp.where(some, top[mid_rows] + jnp.log2(safe), NEG)
        side = jnp.zeros((64, SIDE), F32)
        for n in range(2):
            part[g, :, n * HEAD : (n + 1) * HEAD] = local[n * 64 : (n + 1) * 64].astype(BF16)
            side = jnp.where((lane % 8 == n) & (lane < 24), lse[n * 64 : (n + 1) * 64], side)
        hi = side.astype(BF16).astype(F32)
        mid = (side - hi).astype(BF16).astype(F32)
        low = side - hi - mid
        part[g, :, 2 * HEAD :] = jnp.where(lane < 8, hi, jnp.where(lane < 16, mid, low)).astype(BF16)
        for j in (3, 2, 1):
            src = part.at[g, rows(partner(z, j), 16)]
            rs2[g, j] = start(copy(src, part_in.at[g, j], (rs2_s, rs2_r), 4 * g + j, on_plane(0, j)))

    ag2 = {}
    for g in range(2):
        for j in (1, 2, 3):
            arrived(rs2[g, j])
        pieces = [part[g, rows(z, 16), :].astype(F32)] + [part_in[g, j].astype(F32) for j in (1, 2, 3)]
        lses = []
        for p in pieces:
            s = p[:, 2 * HEAD :]
            lses.append(s + pltpu.roll(s, SIDE - 8, 1) + pltpu.roll(s, SIDE - 16, 1))
        best = functools.reduce(jnp.maximum, lses)
        shares = [jnp.exp2(s - best) for s in lses]
        norm = functools.reduce(jnp.add, shares)
        shares = [s / norm for s in shares]
        merged = []
        for n in range(2):
            terms = [s[:, n : n + 1] * p[:, n * HEAD : (n + 1) * HEAD] for s, p in zip(shares, pieces)]
            merged.append(functools.reduce(jnp.add, terms).astype(BF16))
        att[g, rows(block, 16), :] = jnp.concatenate(merged, axis=1)
        for i, j in PLANE:
            piece = att.at[g, rows(block, 16)]
            ag2[g, i, j] = start(copy(piece, piece, (ag2_s, ag2_r), 16 * g + i * 4 + j, on_plane(i, j)))

    def weights(core, g):
        return ow[pl.ds(pl.multiple_of(core * WIDE + g * 256, 256), 256), :]

    c2 = []
    for g in range(2):
        for i, j in PLANE[::-1]:
            arrived(ag2[g, i, j])
        c2.append(start(copy(att.at[g], att_sib.at[g], (c2_s, c2_r), g, sibling)))
        if g == 0:
            o_sum[...] = jnp.dot(att[0], weights(c, 0), preferred_element_type=F32)
    arrived(c2[0])
    o_sum[...] += jnp.dot(att[1], weights(c, 1), preferred_element_type=F32) + jnp.dot(att_sib[0], weights(1 - c, 0), preferred_element_type=F32)
    arrived(c2[1])
    o_all = o_sum[...] + jnp.dot(att_sib[1], weights(1 - c, 1), preferred_element_type=F32)
    o_sum[...] = o_all
    o_part[...] = o_all.astype(BF16)
    rs3 = {}
    for i, j in OUTER:
        rs3[i, j] = start(copy(o_part.at[rows(outer(i, j), 32)], o_in.at[i * 4 + j], (rs3_s, rs3_r), i * 4 + j, on_outer(i, j)))
    here = rows(head * 4 + tp, 32)
    result = ts[here, :].astype(F32) + o_sum[here, :]
    for i, j in OUTER[::-1]:
        arrived(rs3[i, j])
        result = result + o_in[i * 4 + j].astype(F32)
    out[...] = result.astype(BF16)
    for cp in started:
        cp.wait_send()


def shards(text_states, q_weight, q_gain, visual_key_cache, visual_value_cache, block_mask, lengths, o_weight):
    vmem = pl.BlockSpec(memory_space=pltpu.VMEM)
    hbm = pl.BlockSpec(memory_space=pltpu.HBM)
    dma = pltpu.SemaphoreType.DMA
    return pl.pallas_call(
        kernel,
        out_shape=jax.ShapeDtypeStruct((32, 256), BF16),
        in_specs=[hbm] * 8,
        out_specs=vmem,
        scratch_shapes=[
            pltpu.VMEM((1, HEAD), F32),
            pltpu.VMEM((2, 256), jnp.int32),
            pltpu.VMEM((1, 256), jnp.int32),
            pltpu.VMEM((256, 256), BF16),
            pltpu.VMEM((256, 2 * WIDE), BF16),
            pltpu.VMEM((2 * WIDE, 256), BF16),
            pltpu.VMEM((256, WIDE), F32),
            pltpu.VMEM((256, WIDE), F32),
            pltpu.VMEM((256, WIDE), F32),
            pltpu.VMEM((256, WIDE), jnp.int16),
            pltpu.VMEM((16, 1, 128), F32),
            pltpu.VMEM((16, 16, WIDE), jnp.int16),
            pltpu.VMEM((16, 1, 128), F32),
            pltpu.VMEM((64, WIDE), BF16),
            pltpu.VMEM((8, 512, HEAD), BF16),
            pltpu.VMEM((8, 512, HEAD), BF16),
            pltpu.VMEM((256, SIDE), BF16),
            pltpu.VMEM((8, 64, SIDE), BF16),
            pltpu.VMEM((HEADS * 64, 4096), F32),
            pltpu.VMEM((2, 64, 2 * HEAD + SIDE), BF16),
            pltpu.VMEM((2, 4, 16, 2 * HEAD + SIDE), BF16),
            pltpu.VMEM((2, 256, 2 * HEAD), BF16),
            pltpu.VMEM((2, 256, 2 * HEAD), BF16),
            pltpu.VMEM((256, 256), F32),
            pltpu.VMEM((256, 256), BF16),
            pltpu.VMEM((8, 32, 256), BF16),
            dma((4,)), dma((4,)),
            dma((32,)), dma((32,)),
            dma((15,)), dma((15,)),
            dma((12,)), dma((12,)),
            dma((4,)), dma((4,)),
            dma((8,)), dma((8,)),
            dma((32,)), dma((32,)),
            dma((2,)), dma((2,)),
            dma((8,)), dma((8,)),
            dma((8,)),
        ],
        compiler_params=pltpu.CompilerParams(collective_id=0, has_side_effects=True, vmem_limit_bytes=40 * 1024 * 1024),
    )(*[pltpu.with_memory_space_constraint(a, pltpu.HBM) for a in (text_states, q_weight, q_gain.reshape(1, HEAD), visual_key_cache, visual_value_cache, block_mask.T, lengths.reshape(1, 256), o_weight)])


def solution(mesh):
    in_specs = (
        P(None, "ctx"),
        P("ctx", ("head", "tp")),
        P(),
        P("ctx", ("head", "tp")),
        P("ctx", ("head", "tp")),
        P(None, "ctx"),
        P(),
        P(("head", "tp"), "ctx"),
    )
    out_specs = P(("head", "tp"), "ctx")
    return jax.shard_map(shards, mesh=mesh, in_specs=in_specs, out_specs=out_specs, check_vma=False)
```

```python
import functools

import jax
import jax.numpy as jnp
from jax import lax
from jax.experimental import pallas as pl
from jax.experimental.pallas import tpu as pltpu
from jax.sharding import PartitionSpec as P

MESH = pl.DeviceIdType.MESH
F32, BF16 = jnp.float32, jnp.bfloat16
HEAD = 128
HEADS = 4
WIDE = HEADS * HEAD
SIDE = 128
NEG = -1e30
FLOOR = -1e20
TINY = 1e-30
STEPS = 32000.0
LOG2E = 1.4426950408889634
PLANE = ((2, 3), (2, 2), (1, 3), (3, 3), (1, 2), (3, 2), (0, 3), (0, 2), (2, 1), (1, 1), (3, 1), (2, 0), (0, 1), (1, 0), (3, 0))
OUTER = ((1, 2), (1, 1), (1, 3), (1, 0), (0, 2), (0, 1), (0, 3))


def partner(v, i):
    return (v, v + 1 - 2 * (v % 2), (v + 2) % 4, 3 - v)[i]


def kernel(
    ts_hbm, qw_hbm, gain_hbm, keys, values, seen_hbm, length_hbm, ow_hbm, out,
    gain, seen, length, ts, qw, ow, q_mine, q_other, q_sib, q_part, q_pow, q_in, pow_in, q_rows, kb, vb, mark, marks, scores, part, part_in, att, att_sib, o_sum, o_part, o_in,
    swap_s, swap_r, rs1_s, rs1_r, kv_s, kv_r, fw_s, fw_r, ag1_s, ag1_r, rs2_s, rs2_r, ag2_s, ag2_r, c2_s, c2_r, rs3_s, rs3_r, load,
):
    ctx, head, tp = lax.axis_index("ctx"), lax.axis_index("head"), lax.axis_index("tp")
    x, z, c = ctx // 8, (ctx // 2) % 4, ctx % 2
    block = ctx // 2

    def chip(i, j):
        return partner(x, i) * 4 + partner(z, j)

    def on_plane(i, j):
        return (chip(i, j) * 2 + c, head, tp)

    sibling = (block * 2 + 1 - c, head, tp)

    def outer(i, j):
        return (head + i - 2 * i * head) * 4 + partner(tp, j)

    def on_outer(i, j):
        return (ctx, head + i - 2 * i * head, partner(tp, j))

    def copy(src, dst, sems, slot, device):
        return pltpu.make_async_remote_copy(
            src_ref=src, dst_ref=dst, send_sem=sems[0].at[slot], recv_sem=sems[1].at[slot], device_id=device, device_id_type=MESH
        )

    def rows(i, n):
        return pl.ds(pl.multiple_of(i * n, n), n)

    started = []

    def start(cp):
        cp.start()
        started.append(cp)
        return cp

    def arrived(cp):
        cp.wait_recv()

    def loaded(n):
        loads[n].wait()

    barrier = pltpu.get_barrier_semaphore()
    everyone = [on_outer(i, j) for i, j in OUTER] + [on_plane(i, j) for i, j in PLANE] + [sibling]
    for device in everyone:
        pl.semaphore_signal(barrier, inc=1, device_id=device, device_id_type=MESH)

    mine = pl.ds(pl.multiple_of(c * WIDE, WIDE), WIDE)
    other = pl.ds(pl.multiple_of((1 - c) * WIDE, WIDE), WIDE)
    loads = [
        pltpu.make_async_copy(ts_hbm, ts, load.at[0]),
        pltpu.make_async_copy(qw_hbm, qw, load.at[1]),
        pltpu.make_async_copy(keys, kb.at[0], load.at[2]),
        pltpu.make_async_copy(values, vb.at[0], load.at[3]),
        pltpu.make_async_copy(ow_hbm, ow, load.at[4]),
        pltpu.make_async_copy(gain_hbm, gain, load.at[5]),
        pltpu.make_async_copy(seen_hbm, seen, load.at[6]),
        pltpu.make_async_copy(length_hbm, length, load.at[7]),
    ]
    for cp in loads:
        cp.start()
    loaded(6)
    row = lax.broadcasted_iota(jnp.int32, (256, 256), 0)
    col = lax.broadcasted_iota(jnp.int32, (256, 256), 1)
    lane = lax.broadcasted_iota(jnp.int32, (256, SIDE), 1)
    flags = [jnp.sum(jnp.where(row == col, seen[n : n + 1, :].astype(F32), 0.0), axis=1, keepdims=True) for n in (0, 1)]
    mark[...] = jnp.where(lane == 0, flags[0], jnp.where(lane == 1, flags[1], 0.0)).astype(BF16)
    loaded(0)
    loaded(1)
    q_mine[...] = jnp.dot(ts[...], qw[:, mine], preferred_element_type=F32)
    q_other[...] = jnp.dot(ts[...], qw[:, other], preferred_element_type=F32)

    pl.semaphore_wait(barrier, len(everyone))

    halves = {}
    for i in (0, 2, 1, 3):
        part_rows = rows(partner(x, i), 64)
        halves[i] = start(copy(q_other.at[part_rows], q_sib.at[part_rows], (swap_s, swap_r), i, sibling))

    kv = {}

    bufs = ((keys, kb), (values, vb), (mark, marks))

    def of(ref, what, i):
        return ref.at[rows(partner(x, i), 64)] if what == 2 else ref

    def spread(what):
        src, dst = bufs[what]
        for i in (2, 1, 3) if what == 2 else (1, 3):
            kv[what, i] = start(copy(of(src, what, i), dst.at[2 * i], (kv_s, kv_r), 5 * what + i, on_plane(i, 0)))
        kv[what, 0] = start(copy(of(src, what, 0), dst.at[1], (fw_s, fw_r), 4 * what, sibling))

    def pass_on(what, partners):
        for i in partners:
            buf = bufs[what][1]
            for cp in (kv[what, i],) if (what, i) in kv else (kv[what, 4], kv[what, 5]):
                arrived(cp)
            kv[what, -i] = start(copy(buf.at[2 * i], buf.at[2 * i + 1], (fw_s, fw_r), 4 * what + i, sibling))

    def relay(what):
        buf = bufs[what][1]
        for n, i, lo in ((4, 3, 0), (5, 1, 256)):
            piece = pl.ds(lo, 256)
            kv[what, n] = start(copy(buf.at[2 * i, piece], buf.at[4, piece], (kv_s, kv_r), 5 * what + (0 if n == 4 else 4), on_plane(4 - i, 0)))

    spread(0)

    diagonal = lax.broadcasted_iota(jnp.int32, (16, 128), 0) == lax.broadcasted_iota(jnp.int32, (16, 128), 1)

    rs1 = {}
    for i in (0, 2, 1, 3):
        arrived(halves[i])
        part_rows = rows(partner(x, i), 64)
        q = q_mine[part_rows, :] + q_sib[part_rows, :]
        power = jnp.ceil(jnp.log2(jnp.maximum(jnp.max(jnp.abs(q), axis=1, keepdims=True), TINY)))
        q_part[part_rows, :] = jnp.round(q * (STEPS * jnp.exp2(-power))).astype(jnp.int32).astype(jnp.int16)
        for n in range(4):
            laid = jnp.where(diagonal, power[16 * n : 16 * n + 16], 0.0)
            q_pow[partner(x, i) * 4 + n] = jnp.sum(laid, axis=0, keepdims=True)
        for j in (3, 2, 1, 0):
            if (i, j) != (0, 0):
                src = q_part.at[rows(chip(i, j), 16)]
                rs1[i, j] = start(copy(src, q_in.at[i * 4 + j], (rs1_s, rs1_r), i * 4 + j, on_plane(i, j)))
                src = q_pow.at[chip(i, j)]
                rs1[j, i, 1] = start(copy(src, pow_in.at[i * 4 + j], (rs1_s, rs1_r), 16 + i * 4 + j, on_plane(i, j)))
    spread(1)
    spread(2)
    pass_on(0, (1, 3))
    relay(0)

    def decoded(coded, powers):
        power = jnp.sum(jnp.where(diagonal, powers, 0.0), axis=1, keepdims=True)
        return coded.astype(jnp.int32).astype(F32) * (jnp.exp2(power) / STEPS)

    q_own = decoded(q_part[rows(block, 16), :], q_pow[block])
    for i, j in PLANE[::-1]:
        arrived(rs1[i, j])
        arrived(rs1[j, i, 1])
        q_own = q_own + decoded(q_in[i * 4 + j], pow_in[i * 4 + j])
    normed = []
    loaded(5)
    for n in range(HEADS):
        q = q_own[:, n * HEAD : (n + 1) * HEAD]
        mean_sq = jnp.mean(q * q, axis=-1, keepdims=True)
        normed.append((q * lax.rsqrt(mean_sq + 1e-05) * gain[...]).astype(BF16))
    q_rows[rows(z, 16), :] = jnp.concatenate(normed, axis=1)

    ag1 = [start(copy(q_rows.at[rows(z, 16)], q_rows.at[rows(z, 16)], (ag1_s, ag1_r), j, on_plane(0, j))) for j in (3, 2, 1)]

    pass_on(1, (1, 3))
    relay(1)
    pass_on(2, (1, 3, 2))
    pass_on(0, (2,))

    loaded(7)
    row = lax.broadcasted_iota(jnp.int32, (64, 256), 0) + x * 64
    col = lax.broadcasted_iota(jnp.int32, (64, 256), 1)
    reach = jnp.sum(jnp.where(row == col, length[...].astype(F32), 0.0), axis=1, keepdims=True)
    token = lax.broadcasted_iota(jnp.int32, (64, 256), 1)

    for n in (2, 3, 4):
        loaded(n)
    for what in (0, 2):
        for i in (0, -2, -1, -3):
            arrived(kv[what, i])
    for cp in ag1:
        arrived(cp)
    token_f = token.astype(F32)
    q4 = jnp.concatenate([q_rows[:, n * HEAD : (n + 1) * HEAD] for n in range(HEADS)], axis=0)
    top = jnp.full((4 * 64, 128), NEG, F32)
    for slot in range(8):
        i, d = slot // 2, slot % 2
        k = kb[slot]
        flag = (mark[rows(x, 64), :] if slot == 0 else marks[slot]).astype(F32)
        s = lax.dot_general(q4, k, (((1,), (1,)), ((), ())), preferred_element_type=F32) * (LOG2E / HEAD**0.5)
        first = (chip(i, 0) * 2 + (c if d == 0 else 1 - c)) * 512
        for seg in range(2):
            limit = jnp.where(flag[:, seg : seg + 1] > 0.5, reach, 0.0) - (first + seg * 256).astype(F32)
            ok = token_f < limit
            allowed = jnp.where(ok[None], s[:, seg * 256 : (seg + 1) * 256].reshape(HEADS, 64, 256), NEG).reshape(HEADS * 64, 256)
            scores[:, slot * 512 + seg * 256 : slot * 512 + (seg + 1) * 256] = allowed
            top = jnp.maximum(top, jnp.maximum(allowed[:, :128], allowed[:, 128:]))
    pass_on(1, (2,))
    for i in (0, -1, -3):
        arrived(kv[1, i])
    top = jnp.maximum(jnp.max(top, axis=1, keepdims=True), FLOOR)
    ones = jnp.ones((512, HEAD), BF16)
    lane = lax.broadcasted_iota(jnp.int32, (64, SIDE), 1)
    rs2 = {}
    for g in range(2):
        mid_rows = slice(g * 128, (g + 1) * 128)
        acc = jnp.zeros((128, 2 * HEAD), F32)
        for slot in (0, 1, 2, 6, 3, 7, 5, 4):
            if g == 0 and slot == 5:
                arrived(kv[1, -2])
            w = jnp.exp2(scores[mid_rows, slot * 512 : (slot + 1) * 512] - top[mid_rows]).astype(BF16)
            acc = acc + jnp.dot(w, jnp.concatenate([vb[slot], ones], axis=1), preferred_element_type=F32)
        total = acc[:, HEAD:]
        some = total > 0.0
        safe = jnp.where(some, total, 1.0)
        local = acc[:, :HEAD] / safe
        lse = jnp.where(some, top[mid_rows] + jnp.log2(safe), NEG)
        side = jnp.zeros((64, SIDE), F32)
        for n in range(2):
            part[g, :, n * HEAD : (n + 1) * HEAD] = local[n * 64 : (n + 1) * 64].astype(BF16)
            side = jnp.where((lane % 8 == n) & (lane < 24), lse[n * 64 : (n + 1) * 64], side)
        hi = side.astype(BF16).astype(F32)
        mid = (side - hi).astype(BF16).astype(F32)
        low = side - hi - mid
        part[g, :, 2 * HEAD :] = jnp.where(lane < 8, hi, jnp.where(lane < 16, mid, low)).astype(BF16)
        for j in (3, 2, 1):
            src = part.at[g, rows(partner(z, j), 16)]
            rs2[g, j] = start(copy(src, part_in.at[g, j], (rs2_s, rs2_r), 4 * g + j, on_plane(0, j)))

    ag2 = {}
    for g in range(2):
        for j in (1, 2, 3):
            arrived(rs2[g, j])
        pieces = [part[g, rows(z, 16), :].astype(F32)] + [part_in[g, j].astype(F32) for j in (1, 2, 3)]
        lses = []
        for p in pieces:
            s = p[:, 2 * HEAD :]
            lses.append(s + pltpu.roll(s, SIDE - 8, 1) + pltpu.roll(s, SIDE - 16, 1))
        best = functools.reduce(jnp.maximum, lses)
        shares = [jnp.exp2(s - best) for s in lses]
        norm = functools.reduce(jnp.add, shares)
        shares = [s / norm for s in shares]
        merged = []
        for n in range(2):
            terms = [s[:, n : n + 1] * p[:, n * HEAD : (n + 1) * HEAD] for s, p in zip(shares, pieces)]
            merged.append(functools.reduce(jnp.add, terms).astype(BF16))
        att[g, rows(block, 16), :] = jnp.concatenate(merged, axis=1)
        for i, j in PLANE:
            piece = att.at[g, rows(block, 16)]
            ag2[g, i, j] = start(copy(piece, piece, (ag2_s, ag2_r), 16 * g + i * 4 + j, on_plane(i, j)))

    def weights(core, g):
        return ow[pl.ds(pl.multiple_of(core * WIDE + g * 256, 256), 256), :]

    c2 = []
    for g in range(2):
        for i, j in PLANE[::-1]:
            arrived(ag2[g, i, j])
        c2.append(start(copy(att.at[g], att_sib.at[g], (c2_s, c2_r), g, sibling)))
        if g == 0:
            o_sum[...] = jnp.dot(att[0], weights(c, 0), preferred_element_type=F32)
    arrived(c2[0])
    o_sum[...] += jnp.dot(att[1], weights(c, 1), preferred_element_type=F32) + jnp.dot(att_sib[0], weights(1 - c, 0), preferred_element_type=F32)
    arrived(c2[1])
    o_all = o_sum[...] + jnp.dot(att_sib[1], weights(1 - c, 1), preferred_element_type=F32)
    o_sum[...] = o_all
    o_part[...] = o_all.astype(BF16)
    rs3 = {}
    for i, j in OUTER:
        rs3[i, j] = start(copy(o_part.at[rows(outer(i, j), 32)], o_in.at[i * 4 + j], (rs3_s, rs3_r), i * 4 + j, on_outer(i, j)))
    here = rows(head * 4 + tp, 32)
    result = ts[here, :].astype(F32) + o_sum[here, :]
    for i, j in OUTER[::-1]:
        arrived(rs3[i, j])
        result = result + o_in[i * 4 + j].astype(F32)
    out[...] = result.astype(BF16)
    for cp in started:
        cp.wait_send()


def shards(text_states, q_weight, q_gain, visual_key_cache, visual_value_cache, block_mask, lengths, o_weight):
    vmem = pl.BlockSpec(memory_space=pltpu.VMEM)
    hbm = pl.BlockSpec(memory_space=pltpu.HBM)
    dma = pltpu.SemaphoreType.DMA
    return pl.pallas_call(
        kernel,
        out_shape=jax.ShapeDtypeStruct((32, 256), BF16),
        in_specs=[hbm] * 8,
        out_specs=vmem,
        scratch_shapes=[
            pltpu.VMEM((1, HEAD), F32),
            pltpu.VMEM((2, 256), jnp.int32),
            pltpu.VMEM((1, 256), jnp.int32),
            pltpu.VMEM((256, 256), BF16),
            pltpu.VMEM((256, 2 * WIDE), BF16),
            pltpu.VMEM((2 * WIDE, 256), BF16),
            pltpu.VMEM((256, WIDE), F32),
            pltpu.VMEM((256, WIDE), F32),
            pltpu.VMEM((256, WIDE), F32),
            pltpu.VMEM((256, WIDE), jnp.int16),
            pltpu.VMEM((16, 1, 128), F32),
            pltpu.VMEM((16, 16, WIDE), jnp.int16),
            pltpu.VMEM((16, 1, 128), F32),
            pltpu.VMEM((64, WIDE), BF16),
            pltpu.VMEM((8, 512, HEAD), BF16),
            pltpu.VMEM((8, 512, HEAD), BF16),
            pltpu.VMEM((256, SIDE), BF16),
            pltpu.VMEM((8, 64, SIDE), BF16),
            pltpu.VMEM((HEADS * 64, 4096), F32),
            pltpu.VMEM((2, 64, 2 * HEAD + SIDE), BF16),
            pltpu.VMEM((2, 4, 16, 2 * HEAD + SIDE), BF16),
            pltpu.VMEM((2, 256, 2 * HEAD), BF16),
            pltpu.VMEM((2, 256, 2 * HEAD), BF16),
            pltpu.VMEM((256, 256), F32),
            pltpu.VMEM((256, 256), BF16),
            pltpu.VMEM((8, 32, 256), BF16),
            dma((4,)), dma((4,)),
            dma((32,)), dma((32,)),
            dma((15,)), dma((15,)),
            dma((12,)), dma((12,)),
            dma((4,)), dma((4,)),
            dma((8,)), dma((8,)),
            dma((32,)), dma((32,)),
            dma((2,)), dma((2,)),
            dma((8,)), dma((8,)),
            dma((8,)),
        ],
        compiler_params=pltpu.CompilerParams(collective_id=0, has_side_effects=True, vmem_limit_bytes=40 * 1024 * 1024),
    )(*[pltpu.with_memory_space_constraint(a, pltpu.HBM) for a in (text_states, q_weight, q_gain.reshape(1, HEAD), visual_key_cache, visual_value_cache, block_mask.T, lengths.reshape(1, 256), o_weight)])


def solution(mesh):
    in_specs = (
        P(None, "ctx"),
        P("ctx", ("head", "tp")),
        P(),
        P("ctx", ("head", "tp")),
        P("ctx", ("head", "tp")),
        P(None, "ctx"),
        P(),
        P(("head", "tp"), "ctx"),
    )
    out_specs = P(("head", "tp"), "ctx")
    return jax.shard_map(shards, mesh=mesh, in_specs=in_specs, out_specs=out_specs, check_vma=False)
```

```python
import functools

import jax
import jax.numpy as jnp
from jax import lax
from jax.experimental import pallas as pl
from jax.experimental.pallas import tpu as pltpu
from jax.sharding import PartitionSpec as P

MESH = pl.DeviceIdType.MESH
F32, BF16 = jnp.float32, jnp.bfloat16
HEAD = 128
HEADS = 4
WIDE = HEADS * HEAD
SIDE = 128
NEG = -1e30
FLOOR = -1e20
TINY = 1e-30
STEPS = 32000.0
LOG2E = 1.4426950408889634
PLANE = ((2, 3), (2, 2), (1, 3), (3, 3), (1, 2), (3, 2), (0, 3), (0, 2), (2, 1), (1, 1), (3, 1), (2, 0), (0, 1), (1, 0), (3, 0))
OUTER = ((1, 2), (1, 1), (1, 3), (1, 0), (0, 2), (0, 1), (0, 3))


def partner(v, i):
    return (v, v + 1 - 2 * (v % 2), (v + 2) % 4, 3 - v)[i]


def kernel(
    ts_hbm, qw_hbm, gain_hbm, keys, values, seen_hbm, length_hbm, ow_hbm, out,
    gain, seen, length, ts, qw, ow, q_mine, q_other, q_sib, q_part, q_pow, q_in, pow_in, q_rows, kb, vb, mark, marks, scores, part, part_in, att, att_sib, o_sum, o_part, o_in,
    swap_s, swap_r, rs1_s, rs1_r, kv_s, kv_r, fw_s, fw_r, ag1_s, ag1_r, rs2_s, rs2_r, ag2_s, ag2_r, c2_s, c2_r, rs3_s, rs3_r, load,
):
    ctx, head, tp = lax.axis_index("ctx"), lax.axis_index("head"), lax.axis_index("tp")
    x, z, c = ctx // 8, (ctx // 2) % 4, ctx % 2
    block = ctx // 2

    def chip(i, j):
        return partner(x, i) * 4 + partner(z, j)

    def on_plane(i, j):
        return (chip(i, j) * 2 + c, head, tp)

    sibling = (block * 2 + 1 - c, head, tp)

    def outer(i, j):
        return (head + i - 2 * i * head) * 4 + partner(tp, j)

    def on_outer(i, j):
        return (ctx, head + i - 2 * i * head, partner(tp, j))

    def copy(src, dst, sems, slot, device):
        return pltpu.make_async_remote_copy(
            src_ref=src, dst_ref=dst, send_sem=sems[0].at[slot], recv_sem=sems[1].at[slot], device_id=device, device_id_type=MESH
        )

    def rows(i, n):
        return pl.ds(pl.multiple_of(i * n, n), n)

    started = []

    def start(cp):
        cp.start()
        started.append(cp)
        return cp

    def arrived(cp):
        cp.wait_recv()

    def loaded(n):
        loads[n].wait()

    barrier = pltpu.get_barrier_semaphore()
    everyone = [on_outer(i, j) for i, j in OUTER] + [on_plane(i, j) for i, j in PLANE] + [sibling]
    for device in everyone:
        pl.semaphore_signal(barrier, inc=1, device_id=device, device_id_type=MESH)

    mine = pl.ds(pl.multiple_of(c * WIDE, WIDE), WIDE)
    other = pl.ds(pl.multiple_of((1 - c) * WIDE, WIDE), WIDE)
    loads = [
        pltpu.make_async_copy(ts_hbm, ts, load.at[0]),
        pltpu.make_async_copy(qw_hbm, qw, load.at[1]),
        pltpu.make_async_copy(keys, kb.at[0], load.at[2]),
        pltpu.make_async_copy(values, vb.at[0], load.at[3]),
        pltpu.make_async_copy(ow_hbm, ow, load.at[4]),
        pltpu.make_async_copy(gain_hbm, gain, load.at[5]),
        pltpu.make_async_copy(seen_hbm, seen, load.at[6]),
        pltpu.make_async_copy(length_hbm, length, load.at[7]),
    ]
    for cp in loads:
        cp.start()
    loaded(6)
    row = lax.broadcasted_iota(jnp.int32, (256, 256), 0)
    col = lax.broadcasted_iota(jnp.int32, (256, 256), 1)
    lane = lax.broadcasted_iota(jnp.int32, (256, SIDE), 1)
    flags = [jnp.sum(jnp.where(row == col, seen[n : n + 1, :].astype(F32), 0.0), axis=1, keepdims=True) for n in (0, 1)]
    mark[...] = jnp.where(lane == 0, flags[0], jnp.where(lane == 1, flags[1], 0.0)).astype(BF16)
    loaded(0)
    loaded(1)
    q_mine[...] = jnp.dot(ts[...], qw[:, mine], preferred_element_type=F32)
    q_other[...] = jnp.dot(ts[...], qw[:, other], preferred_element_type=F32)

    pl.semaphore_wait(barrier, len(everyone))

    halves = {}
    for i in (0, 2, 1, 3):
        part_rows = rows(partner(x, i), 64)
        halves[i] = start(copy(q_other.at[part_rows], q_sib.at[part_rows], (swap_s, swap_r), i, sibling))

    kv = {}

    bufs = ((keys, kb), (values, vb), (mark, marks))

    def of(ref, what, i):
        return ref.at[rows(partner(x, i), 64)] if what == 2 else ref

    def spread(what):
        src, dst = bufs[what]
        for i in (2, 1, 3) if what == 2 else (1, 3):
            kv[what, i] = start(copy(of(src, what, i), dst.at[i, 0] if what == 2 else dst.at[2 * i], (kv_s, kv_r), 5 * what + i, on_plane(i, 0)))
        kv[what, 0] = start(copy(of(src, what, 0), dst.at[0, 1] if what == 2 else dst.at[1], (fw_s, fw_r), 4 * what, sibling))

    def pass_on(what, partners):
        for i in partners:
            buf = bufs[what][1]
            for cp in (kv[what, i],) if (what, i) in kv else (kv[what, 4], kv[what, 5]):
                arrived(cp)
            kv[what, -i] = start(copy(buf.at[2 * i], buf.at[2 * i + 1], (fw_s, fw_r), 4 * what + i, sibling))

    def relay(what):
        buf = bufs[what][1]
        for n, i, lo in ((4, 3, 0), (5, 1, 256)):
            piece = pl.ds(lo, 256)
            kv[what, n] = start(copy(buf.at[2 * i, piece], buf.at[4, piece], (kv_s, kv_r), 5 * what + (0 if n == 4 else 4), on_plane(4 - i, 0)))

    spread(0)

    diagonal = lax.broadcasted_iota(jnp.int32, (16, 128), 0) == lax.broadcasted_iota(jnp.int32, (16, 128), 1)

    rs1 = {}
    for i in (0, 2, 1, 3):
        arrived(halves[i])
        part_rows = rows(partner(x, i), 64)
        q = q_mine[part_rows, :] + q_sib[part_rows, :]
        power = jnp.ceil(jnp.log2(jnp.maximum(jnp.max(jnp.abs(q), axis=1, keepdims=True), TINY)))
        q_part[part_rows, :] = jnp.round(q * (STEPS * jnp.exp2(-power))).astype(jnp.int32).astype(jnp.int16)
        for n in range(4):
            laid = jnp.where(diagonal, power[16 * n : 16 * n + 16], 0.0)
            q_pow[partner(x, i) * 4 + n] = jnp.sum(laid, axis=0, keepdims=True)
        for j in (3, 2, 1, 0):
            if (i, j) != (0, 0):
                src = q_part.at[rows(chip(i, j), 16)]
                rs1[i, j] = start(copy(src, q_in.at[i * 4 + j], (rs1_s, rs1_r), i * 4 + j, on_plane(i, j)))
                src = q_pow.at[chip(i, j)]
                rs1[j, i, 1] = start(copy(src, pow_in.at[i * 4 + j], (rs1_s, rs1_r), 16 + i * 4 + j, on_plane(i, j)))
    spread(1)
    spread(2)
    pass_on(0, (1, 3))
    relay(0)

    def decoded(coded, powers):
        power = jnp.sum(jnp.where(diagonal, powers, 0.0), axis=1, keepdims=True)
        return coded.astype(jnp.int32).astype(F32) * (jnp.exp2(power) / STEPS)

    q_own = decoded(q_part[rows(block, 16), :], q_pow[block])
    for i, j in PLANE[::-1]:
        arrived(rs1[i, j])
        arrived(rs1[j, i, 1])
        q_own = q_own + decoded(q_in[i * 4 + j], pow_in[i * 4 + j])
    normed = []
    loaded(5)
    for n in range(HEADS):
        q = q_own[:, n * HEAD : (n + 1) * HEAD]
        mean_sq = jnp.mean(q * q, axis=-1, keepdims=True)
        normed.append((q * lax.rsqrt(mean_sq + 1e-05) * gain[...]).astype(BF16))
    q_rows[rows(z, 16), :] = jnp.concatenate(normed, axis=1)

    ag1 = [start(copy(q_rows.at[rows(z, 16)], q_rows.at[rows(z, 16)], (ag1_s, ag1_r), j, on_plane(0, j))) for j in (3, 2, 1)]

    pass_on(1, (1, 3))
    relay(1)
    for i in (1, 3, 2):
        arrived(kv[2, i])
    kv[2, -1] = start(copy(marks.at[1:4, 0], marks.at[1:4, 1], (fw_s, fw_r), 9, sibling))
    pass_on(0, (2,))

    loaded(7)
    row = lax.broadcasted_iota(jnp.int32, (64, 256), 0) + x * 64
    col = lax.broadcasted_iota(jnp.int32, (64, 256), 1)
    reach = jnp.sum(jnp.where(row == col, length[...].astype(F32), 0.0), axis=1, keepdims=True)
    token = lax.broadcasted_iota(jnp.int32, (64, 256), 1)

    for n in (2, 3, 4):
        loaded(n)
    for i in (0, -2, -1, -3):
        arrived(kv[0, i])
    for i in (0, -1):
        arrived(kv[2, i])
    for cp in ag1:
        arrived(cp)
    token_f = token.astype(F32)
    q4 = jnp.concatenate([q_rows[:, n * HEAD : (n + 1) * HEAD] for n in range(HEADS)], axis=0)
    top = jnp.full((4 * 64, 128), NEG, F32)
    for slot in range(8):
        i, d = slot // 2, slot % 2
        k = kb[slot]
        flag = (mark[rows(x, 64), :] if slot == 0 else marks[slot // 2, slot % 2]).astype(F32)
        s = lax.dot_general(q4, k, (((1,), (1,)), ((), ())), preferred_element_type=F32) * (LOG2E / HEAD**0.5)
        first = (chip(i, 0) * 2 + (c if d == 0 else 1 - c)) * 512
        for seg in range(2):
            limit = jnp.where(flag[:, seg : seg + 1] > 0.5, reach, 0.0) - (first + seg * 256).astype(F32)
            ok = token_f < limit
            allowed = jnp.where(ok[None], s[:, seg * 256 : (seg + 1) * 256].reshape(HEADS, 64, 256), NEG).reshape(HEADS * 64, 256)
            scores[:, slot * 512 + seg * 256 : slot * 512 + (seg + 1) * 256] = allowed
            top = jnp.maximum(top, jnp.maximum(allowed[:, :128], allowed[:, 128:]))
    pass_on(1, (2,))
    for i in (0, -1, -3):
        arrived(kv[1, i])
    top = jnp.maximum(jnp.max(top, axis=1, keepdims=True), FLOOR)
    ones = jnp.ones((512, HEAD), BF16)
    lane = lax.broadcasted_iota(jnp.int32, (64, SIDE), 1)
    rs2 = {}
    for g in range(2):
        mid_rows = slice(g * 128, (g + 1) * 128)
        acc = jnp.zeros((128, 2 * HEAD), F32)
        for slot in (0, 1, 2, 6, 3, 7, 5, 4):
            if g == 0 and slot == 5:
                arrived(kv[1, -2])
            w = jnp.exp2(scores[mid_rows, slot * 512 : (slot + 1) * 512] - top[mid_rows]).astype(BF16)
            acc = acc + jnp.dot(w, jnp.concatenate([vb[slot], ones], axis=1), preferred_element_type=F32)
        total = acc[:, HEAD:]
        some = total > 0.0
        safe = jnp.where(some, total, 1.0)
        local = acc[:, :HEAD] / safe
        lse = jnp.where(some, top[mid_rows] + jnp.log2(safe), NEG)
        side = jnp.zeros((64, SIDE), F32)
        for n in range(2):
            part[g, :, n * HEAD : (n + 1) * HEAD] = local[n * 64 : (n + 1) * 64].astype(BF16)
            side = jnp.where((lane % 8 == n) & (lane < 24), lse[n * 64 : (n + 1) * 64], side)
        hi = side.astype(BF16).astype(F32)
        mid = (side - hi).astype(BF16).astype(F32)
        low = side - hi - mid
        part[g, :, 2 * HEAD :] = jnp.where(lane < 8, hi, jnp.where(lane < 16, mid, low)).astype(BF16)
        for j in (3, 2, 1):
            src = part.at[g, rows(partner(z, j), 16)]
            rs2[g, j] = start(copy(src, part_in.at[g, j], (rs2_s, rs2_r), 4 * g + j, on_plane(0, j)))

    ag2 = {}
    for g in range(2):
        for j in (1, 2, 3):
            arrived(rs2[g, j])
        pieces = [part[g, rows(z, 16), :].astype(F32)] + [part_in[g, j].astype(F32) for j in (1, 2, 3)]
        lses = []
        for p in pieces:
            s = p[:, 2 * HEAD :]
            lses.append(s + pltpu.roll(s, SIDE - 8, 1) + pltpu.roll(s, SIDE - 16, 1))
        best = functools.reduce(jnp.maximum, lses)
        shares = [jnp.exp2(s - best) for s in lses]
        norm = functools.reduce(jnp.add, shares)
        shares = [s / norm for s in shares]
        merged = []
        for n in range(2):
            terms = [s[:, n : n + 1] * p[:, n * HEAD : (n + 1) * HEAD] for s, p in zip(shares, pieces)]
            merged.append(functools.reduce(jnp.add, terms).astype(BF16))
        att[g, rows(block, 16), :] = jnp.concatenate(merged, axis=1)
        for i, j in PLANE:
            piece = att.at[g, rows(block, 16)]
            ag2[g, i, j] = start(copy(piece, piece, (ag2_s, ag2_r), 16 * g + i * 4 + j, on_plane(i, j)))

    def weights(core, g):
        return ow[pl.ds(pl.multiple_of(core * WIDE + g * 256, 256), 256), :]

    c2 = []
    for g in range(2):
        for i, j in PLANE[::-1]:
            arrived(ag2[g, i, j])
        c2.append(start(copy(att.at[g], att_sib.at[g], (c2_s, c2_r), g, sibling)))
        if g == 0:
            o_sum[...] = jnp.dot(att[0], weights(c, 0), preferred_element_type=F32)
    arrived(c2[0])
    o_sum[...] += jnp.dot(att[1], weights(c, 1), preferred_element_type=F32) + jnp.dot(att_sib[0], weights(1 - c, 0), preferred_element_type=F32)
    arrived(c2[1])
    o_all = o_sum[...] + jnp.dot(att_sib[1], weights(1 - c, 1), preferred_element_type=F32)
    o_sum[...] = o_all
    o_part[...] = o_all.astype(BF16)
    rs3 = {}
    for i, j in OUTER:
        rs3[i, j] = start(copy(o_part.at[rows(outer(i, j), 32)], o_in.at[i * 4 + j], (rs3_s, rs3_r), i * 4 + j, on_outer(i, j)))
    here = rows(head * 4 + tp, 32)
    result = ts[here, :].astype(F32) + o_sum[here, :]
    for i, j in OUTER[::-1]:
        arrived(rs3[i, j])
        result = result + o_in[i * 4 + j].astype(F32)
    out[...] = result.astype(BF16)
    for cp in started:
        cp.wait_send()


def shards(text_states, q_weight, q_gain, visual_key_cache, visual_value_cache, block_mask, lengths, o_weight):
    vmem = pl.BlockSpec(memory_space=pltpu.VMEM)
    hbm = pl.BlockSpec(memory_space=pltpu.HBM)
    dma = pltpu.SemaphoreType.DMA
    return pl.pallas_call(
        kernel,
        out_shape=jax.ShapeDtypeStruct((32, 256), BF16),
        in_specs=[hbm] * 8,
        out_specs=vmem,
        scratch_shapes=[
            pltpu.VMEM((1, HEAD), F32),
            pltpu.VMEM((2, 256), jnp.int32),
            pltpu.VMEM((1, 256), jnp.int32),
            pltpu.VMEM((256, 256), BF16),
            pltpu.VMEM((256, 2 * WIDE), BF16),
            pltpu.VMEM((2 * WIDE, 256), BF16),
            pltpu.VMEM((256, WIDE), F32),
            pltpu.VMEM((256, WIDE), F32),
            pltpu.VMEM((256, WIDE), F32),
            pltpu.VMEM((256, WIDE), jnp.int16),
            pltpu.VMEM((16, 1, 128), F32),
            pltpu.VMEM((16, 16, WIDE), jnp.int16),
            pltpu.VMEM((16, 1, 128), F32),
            pltpu.VMEM((64, WIDE), BF16),
            pltpu.VMEM((8, 512, HEAD), BF16),
            pltpu.VMEM((8, 512, HEAD), BF16),
            pltpu.VMEM((256, SIDE), BF16),
            pltpu.VMEM((4, 2, 64, SIDE), BF16),
            pltpu.VMEM((HEADS * 64, 4096), F32),
            pltpu.VMEM((2, 64, 2 * HEAD + SIDE), BF16),
            pltpu.VMEM((2, 4, 16, 2 * HEAD + SIDE), BF16),
            pltpu.VMEM((2, 256, 2 * HEAD), BF16),
            pltpu.VMEM((2, 256, 2 * HEAD), BF16),
            pltpu.VMEM((256, 256), F32),
            pltpu.VMEM((256, 256), BF16),
            pltpu.VMEM((8, 32, 256), BF16),
            dma((4,)), dma((4,)),
            dma((32,)), dma((32,)),
            dma((15,)), dma((15,)),
            dma((12,)), dma((12,)),
            dma((4,)), dma((4,)),
            dma((8,)), dma((8,)),
            dma((32,)), dma((32,)),
            dma((2,)), dma((2,)),
            dma((8,)), dma((8,)),
            dma((8,)),
        ],
        compiler_params=pltpu.CompilerParams(collective_id=0, has_side_effects=True, vmem_limit_bytes=40 * 1024 * 1024),
    )(*[pltpu.with_memory_space_constraint(a, pltpu.HBM) for a in (text_states, q_weight, q_gain.reshape(1, HEAD), visual_key_cache, visual_value_cache, block_mask.T, lengths.reshape(1, 256), o_weight)])


def solution(mesh):
    in_specs = (
        P(None, "ctx"),
        P("ctx", ("head", "tp")),
        P(),
        P("ctx", ("head", "tp")),
        P("ctx", ("head", "tp")),
        P(None, "ctx"),
        P(),
        P(("head", "tp"), "ctx"),
    )
    out_specs = P(("head", "tp"), "ctx")
    return jax.shard_map(shards, mesh=mesh, in_specs=in_specs, out_specs=out_specs, check_vma=False)
```
